32 devices in a mesh: ty: 4 (over y, x), tx: 4 (over z), slide: 2 (over core).
Axes of the slice: x: 2, y: 2, z: 4, core: 2. Of those that a mesh axis runs over, the one named last changes fastest.
Arguments:
- tokens: bfloat16 [8, 4, 192, 768], P(('slide', 'ty'), 'tx'), parts along dimension 0, may hold values from -6 to 6
- summary: bfloat16 [512, 768], P(('slide', 'ty', 'tx')), parts along dimension 0, may hold values from -6 to 6
- counts: int32 [8, 4], P('slide'), parts along dimension 0, may hold values from 1 to 192, as said below
- tile_pattern: int32 [8, 4, 9], P('slide'), parts along dimension 0, may hold values from 0 to 1, as said below
- summary_pattern: int32 [8, 4, 2], P(('slide', 'ty'), 'tx'), parts along dimension 0, may hold values 0 or 1
- norm_gain: float32 [768], replicated, may hold values from 0.1 to 1.9
- projections: bfloat16 [4, 768, 768], replicated, may hold values from -4 to 4
- cotangent: bfloat16 [8, 4, 192, 768], P(('slide', 'ty'), 'tx'), parts along dimension 0, may hold values from -6 to 6
Outputs:
- updated: bfloat16 [8, 4, 192, 768], P(('slide', 'ty'), 'tx'), parts along dimension 0
- grad_tokens: bfloat16 [8, 4, 192, 768], P(('slide', 'ty'), 'tx'), parts along dimension 0
- grad_summary: bfloat16 [512, 768], P(('slide', 'ty', 'tx')), parts along dimension 0
- grad_proj: float32 [8, 768, 768], P('slide'), parts along dimension 0
- grad_gain: float32 [1536], P('slide'), parts along dimension 0
The draws below stay inside these ranges and needn't reach their ends.
There are 2 independent parts, one for each index of `slide`. The reference program is written for one: setup_inputs(seed, part) draws one part's arguments, and reference() takes and returns one part's arrays. A program takes and returns all parts, laid end to end along the dimension named above; an argument that names none is the same for every part. Nothing has to cross between parts.
Inputs may be any that keep to these rules, and one draw needn't show every extreme that they name: `counts`: some tile holds exactly 192 tokens and some tile exactly 1 in every draw. `tile_pattern`: entry 4, the tile itself, is always 1.
All inputs are finite; a program needn't handle non-finite values. No bound on the sum of `summary_pattern` on one device may be relied on, other than what follows from the above.
Results may differ from the reference program's by a relative error of at most 0.011.
Values may be sent and summed in bfloat16 or wider, within the bound.
No kernel may reach another device: no remote copies, remote signals or barrier semaphores. Data moves between devices by JAX's collectives and lax.ppermute only.
A program may use at most 128 MiB of HBM per device.

```python
import math
import jax
import jax.numpy as jnp
from jax import lax

D = 768
HEADS = 12
TILE = 192
SBLK = 128
SUMMARIES = 256
SUM_BLOCKS = 2
N_TY = 4
N_TX = 4


def draw_counts(key, part):
    draw_one, draw_two, draw_three, draw_four = jax.random.split(jax.random.fold_in(key, 11), 4)
    dense_count = jax.random.randint(draw_one, (N_TY * N_TX,), 1, TILE + 1)
    sparse_count = jax.random.randint(draw_two, (N_TY * N_TX,), 1, TILE // 8 + 1)
    selector = jax.random.randint(draw_three, (N_TY * N_TX,), 0, 4)
    values = jnp.where(selector == 0, sparse_count, dense_count)
    position = jax.random.randint(draw_four, (), 0, N_TY * N_TX)
    values = values.at[position].set(TILE)
    values = values.at[(position + 1) % (N_TY * N_TX)].set(1)
    return values.reshape(N_TY, N_TX).astype(jnp.int32)


def draw_tile_pattern(key, part):
    raw_draws = jax.random.randint(jax.random.fold_in(key, 23), (N_TY, N_TX, 9), 0, 4)
    pattern = (raw_draws > 0).astype(jnp.int32)
    return pattern.at[:, :, 4].set(1)


def draw_projections(key, part):
    draw_one = jax.random.fold_in(jax.random.fold_in(key, 37), 0)
    weights = jax.random.normal(draw_one, (4, D, D), jnp.float32) * D ** (-0.5)
    return jnp.clip(weights, -4.0, 4.0).astype(jnp.bfloat16)


def touch_ends(drawn, rng, smallest, top_value):
    longest = drawn.shape.index(max(drawn.shape))
    spots = []
    for shift in (0, 1):
        where = [jax.random.randint(jax.random.fold_in(rng, axis), (), 0, length) for axis, length in enumerate(drawn.shape)]
        where[longest] = (where[longest] + shift) % drawn.shape[longest]
        spots.append(tuple(where))
    return drawn.at[spots[0]].set(smallest).at[spots[1]].set(top_value)


def steps_of(own_key, dims, cuts, low, high):
    level = 1.0
    for dim, shards_of in cuts:
        draws = jax.random.uniform(jax.random.fold_in(jax.random.fold_in(own_key, 6), dim), (shards_of,), jnp.float32, low / len(cuts), high / len(cuts))
        level = level * jnp.repeat(jnp.exp(draws), dims[dim] // shards_of).reshape((-1,) + (1,) * (len(dims) - 1 - dim))
    return level


def scatter_about(rng, extent, scale, reach, cuts=(), kind=jnp.bfloat16):
    values = jax.random.normal(rng, extent, jnp.float32) * scale
    if len(cuts) > 0:
        values = steps_of(rng, extent, cuts, -0.22, 0.18) * values
    return jnp.clip(values, min=-reach, max=reach).astype(kind)


def setup_inputs(seed: int = 0, part: int = 0) -> dict:
    streams_of = jax.random.split(jax.random.key(seed), 9)
    part_splits = jax.random.split(jax.random.fold_in(streams_of[8], part), 9)
    tokens = scatter_about(part_splits[0], (N_TY, N_TX, TILE, D), 1.0, 6.0, ((0, 4), (1, 4)))
    summary = scatter_about(part_splits[1], (SUMMARIES, D), 1.0, 6.0, ((0, 16),))
    counts = draw_counts(jax.random.fold_in(jax.random.fold_in(streams_of[8], part), 71), part)
    tile_pattern = draw_tile_pattern(jax.random.fold_in(jax.random.fold_in(streams_of[8], part), 71), part)
    summary_pattern = touch_ends((jax.random.randint(part_splits[4], (N_TY, N_TX, SUM_BLOCKS), 0, 4) < 3).astype(jnp.int32), jax.random.fold_in(part_splits[4], 1), 0, 1)
    norm_gain = jnp.clip(1.0 + 0.18 * jax.random.normal(streams_of[5], (D,), jnp.float32), 0.1, 1.9)
    projections = draw_projections(jax.random.fold_in(streams_of[8], 71), part)
    cotangent = scatter_about(part_splits[7], (N_TY, N_TX, TILE, D), 1.0, 6.0, ((0, 4), (1, 4)))
    return dict(tokens=tokens, summary=summary, counts=counts, tile_pattern=tile_pattern, summary_pattern=summary_pattern, norm_gain=norm_gain, projections=projections, cotangent=cotangent)


epsilon = 1e-05

def rounded(values):
    return lax.optimization_barrier(values.astype(jnp.bfloat16)).astype(jnp.float32)

def normalize(rows, gain):
    values = rows.astype(jnp.float32)
    scale = lax.rsqrt(lax.optimization_barrier(jnp.mean(values * values, axis=-1, keepdims=True)) + epsilon)
    return ((values * scale * gain).astype(jnp.bfloat16), scale)

def norm_back(rows, scale, gain, grad_norm):
    values = rows.astype(jnp.float32)
    scaled = gain * grad_norm
    return scale * scaled - values * scale ** 3 * lax.optimization_barrier(jnp.mean(values * scaled, axis=-1, keepdims=True))

def project(rows, weight):
    return jnp.dot(rows, weight, preferred_element_type=jnp.float32).astype(jnp.bfloat16)

def back_project(rows, weight):
    return jnp.dot(rows, weight.T, preferred_element_type=jnp.float32)

def exact_back(rows, weight):
    return jnp.dot(rows, weight.astype(jnp.float32).T, precision=lax.Precision.HIGHEST)

def contract_rows(left, right):
    return lax.dot_general(left, right, (((0,), (0,)), ((), ())), preferred_element_type=jnp.float32)

def exact_rows(left, right):
    return lax.dot_general(left.astype(jnp.float32), right, (((0,), (0,)), ((), ())), precision=lax.Precision.HIGHEST)

def reference(tokens, summary, counts, tile_pattern, summary_pattern, norm_gain, projections, cotangent):
    head_size = D // HEADS
    factor = 1.0 / math.sqrt(head_size)
    near_rows = 9 * TILE
    total_keys = near_rows + SUMMARIES
    token_rows = tokens.reshape(-1, D)
    hidden, row_scale = normalize(token_rows, norm_gain)
    summary_hidden, summary_scale = normalize(summary, norm_gain)
    w_query, w_key, w_value, w_out = (projections[0], projections[1], projections[2], projections[3])
    grid_shape = (N_TY, N_TX, TILE, D)
    queries = project(hidden, w_query).reshape(grid_shape)
    keys = project(hidden, w_key).reshape(grid_shape)
    values = project(hidden, w_value).reshape(grid_shape)
    summary_keys = project(summary_hidden, w_key)
    summary_values = project(summary_hidden, w_value)
    grid_pad = ((1, 1), (1, 1), (0, 0), (0, 0))
    key_pad = jnp.pad(keys, grid_pad)
    value_pad = jnp.pad(values, grid_pad)
    count_pad = jnp.pad(counts, 1)
    positions = jnp.arange(TILE, dtype=jnp.int32)

    def visit_tile(running, tile_index):
        grid_kgrad, grid_vgrad, summ_kgrad, summ_vgrad, out_grad = running
        zero = jnp.zeros((), jnp.int32)
        grid_row = (tile_index // N_TX).astype(jnp.int32)
        grid_col = (tile_index % N_TX).astype(jnp.int32)
        corner = (grid_row, grid_col, zero, zero)
        near_keys = lax.dynamic_slice(key_pad, corner, (3, 3, TILE, D)).reshape(near_rows, D)
        near_values = lax.dynamic_slice(value_pad, corner, (3, 3, TILE, D)).reshape(near_rows, D)
        near_counts = lax.dynamic_slice(count_pad, (grid_row, grid_col), (3, 3)).reshape(9)
        tile_flags = lax.dynamic_slice(tile_pattern, (grid_row, grid_col, zero), (1, 1, 9)).reshape(9)
        tile_ok = ((positions[None, :] < near_counts[:, None]) & (tile_flags[:, None] == 1)).reshape(near_rows)
        summ_flags = lax.dynamic_slice(summary_pattern, (grid_row, grid_col, zero), (1, 1, SUMMARIES // SBLK)).reshape(-1)
        summ_ok = jnp.repeat(summ_flags == 1, SBLK)
        allowed = jnp.concatenate([tile_ok, summ_ok])
        all_keys = jnp.concatenate([near_keys, summary_keys]).astype(jnp.float32).reshape(total_keys, HEADS, head_size)
        all_values = jnp.concatenate([near_values, summary_values]).astype(jnp.float32).reshape(total_keys, HEADS, head_size)
        query_here = lax.dynamic_slice(queries, corner, (1, 1, TILE, D)).reshape(TILE, HEADS, head_size).astype(jnp.float32)
        scores = jnp.einsum('qhd,khd->hqk', query_here, all_keys) * factor
        scores = jnp.where(allowed[None, None, :], scores, -jnp.inf)
        largest = lax.optimization_barrier(jnp.max(scores, axis=-1, keepdims=True))
        exponent = jnp.exp(scores - largest)
        denominator = lax.optimization_barrier(jnp.sum(exponent, axis=-1, keepdims=True))
        weights_full = exponent / denominator
        weights_half = rounded(weights_full)
        attended = jnp.einsum('hqk,khd->qhd', weights_half, all_values).reshape(TILE, D).astype(jnp.bfloat16)
        own_count = near_counts[4]
        row_mask = (positions < own_count).astype(jnp.float32)[:, None]
        rows_here = lax.dynamic_slice(tokens, corner, (1, 1, TILE, D)).reshape(TILE, D)
        updated = (rows_here.astype(jnp.float32) + row_mask * jnp.dot(attended, w_out, preferred_element_type=jnp.float32)).astype(jnp.bfloat16)
        grads_here = lax.dynamic_slice(cotangent, corner, (1, 1, TILE, D)).reshape(TILE, D)
        masked = (grads_here.astype(jnp.float32) * row_mask).astype(jnp.bfloat16)
        out_grad = out_grad + contract_rows(attended, masked)
        attended_grad = rounded(back_project(masked, w_out)).reshape(TILE, HEADS, head_size)
        grad_weights = jnp.einsum('qhd,khd->hqk', attended_grad, all_values)
        row_delta = lax.optimization_barrier(jnp.sum(weights_full * grad_weights, axis=-1, keepdims=True))
        grad_scores = rounded(weights_full * (grad_weights - row_delta))
        query_grad = (jnp.einsum('hqk,khd->qhd', grad_scores, all_keys) * factor).reshape(TILE, D).astype(jnp.bfloat16)
        key_grads = (jnp.einsum('hqk,qhd->khd', grad_scores, query_here) * factor).reshape(total_keys, D)
        value_grads = jnp.einsum('hqk,qhd->khd', weights_half, attended_grad).reshape(total_keys, D)
        grid_kgrad = lax.dynamic_update_slice(grid_kgrad, lax.dynamic_slice(grid_kgrad, corner, (3, 3, TILE, D)) + key_grads[:near_rows].reshape(3, 3, TILE, D), corner)
        grid_vgrad = lax.dynamic_update_slice(grid_vgrad, lax.dynamic_slice(grid_vgrad, corner, (3, 3, TILE, D)) + value_grads[:near_rows].reshape(3, 3, TILE, D), corner)
        summ_kgrad = summ_kgrad + key_grads[near_rows:]
        summ_vgrad = summ_vgrad + value_grads[near_rows:]
        return ((grid_kgrad, grid_vgrad, summ_kgrad, summ_vgrad, out_grad), (updated, query_grad))
    start_state = (jnp.zeros((N_TY + 2, N_TX + 2, TILE, D), jnp.float32), jnp.zeros((N_TY + 2, N_TX + 2, TILE, D), jnp.float32), jnp.zeros((SUMMARIES, D), jnp.float32), jnp.zeros((SUMMARIES, D), jnp.float32), jnp.zeros((D, D), jnp.float32))
    final_state, stacked = lax.scan(visit_tile, start_state, jnp.arange(N_TY * N_TX, dtype=jnp.int32))
    grid_kgrad, grid_vgrad, summ_kgrad, summ_vgrad, out_grad = final_state
    updated = stacked[0].reshape(tokens.shape)
    query_grad = stacked[1].reshape(-1, D)
    key_grad = grid_kgrad[1:-1, 1:-1].reshape(-1, D).astype(jnp.bfloat16)
    value_grad = grid_vgrad[1:-1, 1:-1].reshape(-1, D).astype(jnp.bfloat16)
    summary_key_grad = summ_kgrad
    summary_value_grad = summ_vgrad
    hidden_grad = back_project(query_grad, w_query) + back_project(key_grad, w_key) + back_project(value_grad, w_value)
    summary_hidden_grad = exact_back(summary_key_grad, w_key) + exact_back(summary_value_grad, w_value)
    grad_proj = jnp.stack([contract_rows(hidden, query_grad), contract_rows(hidden, key_grad) + exact_rows(summary_hidden, summary_key_grad), contract_rows(hidden, value_grad) + exact_rows(summary_hidden, summary_value_grad), out_grad])
    grad_gain = lax.optimization_barrier(jnp.sum(hidden_grad * token_rows.astype(jnp.float32) * row_scale, axis=0)) + lax.optimization_barrier(jnp.sum(summary_hidden_grad * summary.astype(jnp.float32) * summary_scale, axis=0))
    grad_tokens = (cotangent.reshape(-1, D).astype(jnp.float32) + norm_back(token_rows, row_scale, norm_gain, hidden_grad)).astype(jnp.bfloat16).reshape(tokens.shape)
    grad_summary = norm_back(summary, summary_scale, norm_gain, summary_hidden_grad).astype(jnp.bfloat16)
    return (updated, grad_tokens, grad_summary, grad_proj, grad_gain)
```

```python
import functools
import math

import jax
import jax.numpy as jnp
from jax import lax
from jax.experimental import pallas as pl
from jax.experimental.pallas import tpu as pltpu
from jax.sharding import PartitionSpec as P

HEADS = 12
SBLK = 128
CHUNK = 256
GROUP = 16
FAR = -1e30
epsilon = 1e-05


f32 = jnp.float32
bf16 = jnp.bfloat16


def shifted(array, axis, by):
    peers = lax.axis_size(axis)
    pairs = [(i, i + by) for i in range(peers) if 0 <= i + by < peers]
    return lax.ppermute(array, axis, pairs)


def rotated(array, axis, by):
    peers = lax.axis_size(axis)
    return lax.ppermute(array, axis, [(i, (i + by) % peers) for i in range(peers)])


def swapped(array, axis, bit):
    peers = lax.axis_size(axis)
    return lax.ppermute(array, axis, [(i, i ^ (1 << bit)) for i in range(peers)])


def rms_scale(rows):
    values = rows.astype(f32)
    return lax.rsqrt(jnp.mean(values * values, axis=-1, keepdims=True) + epsilon)


def norm_back(rows, scale, gain, grad_norm):
    values = rows.astype(f32)
    scaled = gain * grad_norm
    return scale * scaled - values * scale**3 * jnp.mean(values * scaled, axis=-1, keepdims=True)


def mm(left, right, contract=((1,), (0,))):
    return lax.dot_general(left, right, (contract, ((), ())), preferred_element_type=f32)


def layer_kernel(segments, n_in, meta, tokens, grads, *refs):
    sources = refs[:n_in]
    wq_ref, wk_ref, wv_ref, wo_ref = refs[n_in : n_in + 4]
    outs = refs[n_in + 4 :]
    updated_ref, dw3_ref, dwo_ref = outs[:3]
    targets = outs[3 : 3 + n_in]
    (hc, hct, own_t, masked, bias, kv_s, e_s, dh_s, ot_s, dqt_s, dwkv_s, upd_s, dhq_s) = outs[
        3 + n_in :
    ]
    own_ref = sources[0]
    step = pl.program_id(0)
    n_seg = len(segments)
    rows = own_ref.shape[0]
    width = own_ref.shape[1]
    half = 64
    factor = 1.0 / math.sqrt(half)
    total = meta[0, n_seg]
    chunks = lax.div(total + (CHUNK - 1), CHUNK)
    own_count = meta[1, n_seg]

    @pl.when(step == 0)
    def _():
        offset = jnp.int32(0)
        for s, (which, start) in enumerate(segments):
            valid = meta[1, s]

            def gather(j, carry, which=which, start=start, valid=valid, offset=offset):
                there = pl.multiple_of(offset + j * GROUP, GROUP)
                here = pl.multiple_of(start + j * GROUP, GROUP)
                hc[pl.ds(there, GROUP), :] = sources[which][pl.ds(here, GROUP), :]
                place = lax.broadcasted_iota(jnp.int32, (GROUP, 128), 0) + j * GROUP
                bias[pl.ds(there, GROUP), :] = jnp.where(place < valid, 0.0, FAR)
                return carry

            lax.fori_loop(0, meta[0, s], gather, 0)
            offset = offset + meta[0, s] * GROUP

        def tail(j, carry):
            there = pl.multiple_of(j * GROUP, GROUP)
            hc[pl.ds(there, GROUP), :] = jnp.zeros((GROUP, width), bf16)
            bias[pl.ds(there, GROUP), :] = jnp.full((GROUP, 128), FAR, f32)
            return carry

        lax.fori_loop(lax.div(total, GROUP), chunks * (CHUNK // GROUP), tail, 0)

        def turn(c, carry):
            at = pl.ds(pl.multiple_of(c * CHUNK, CHUNK), CHUNK)
            hct[c] = hc[at, :].T
            dh_s[at, :] = jnp.zeros((CHUNK, width), f32)
            return carry

        lax.fori_loop(0, chunks, turn, 0)
        own_t[...] = own_ref[...].T
        live = lax.broadcasted_iota(jnp.int32, (rows, width), 0) < own_count
        masked[...] = jnp.where(live, grads[...], jnp.zeros_like(grads[...]))
        upd_s[...] = jnp.zeros_like(upd_s)
        dhq_s[...] = jnp.zeros_like(dhq_s)

    wq = wq_ref[0]
    wo = wo_ref[0]
    wkv = jnp.concatenate([wk_ref[0], wv_ref[0]], axis=1)
    low = lax.broadcasted_iota(jnp.int32, (rows, 128), 1) < half
    query = (mm(own_ref[...], wq).astype(bf16) * factor).astype(bf16)
    grad = mm(masked[...], wo, ((1,), (1,))).astype(bf16)
    nil = jnp.zeros_like(query)
    q2 = jnp.concatenate([jnp.where(low, query, nil), jnp.where(low, nil, query)], axis=0)
    g2 = jnp.concatenate([jnp.where(low, grad, nil), jnp.where(low, nil, grad)], axis=0)
    q2t = q2.T
    g2t = g2.T
    lanes = 2 * rows

    def score(c, largest):
        at = pl.ds(pl.multiple_of(c * CHUNK, CHUNK), CHUNK)
        kv = mm(hc[at, :], wkv).astype(bf16)
        kv_s[at, :] = kv
        b = bias[at, :]
        scores = mm(kv[:, :128], q2t) + jnp.concatenate([b] * (lanes // 128), axis=1)
        e_s[at, :] = scores
        return jnp.maximum(largest, jnp.max(scores.reshape(CHUNK // 8, 8, lanes), axis=0))

    largest = lax.fori_loop(0, chunks, score, jnp.full((8, lanes), FAR, f32))
    largest = jnp.max(largest, axis=0, keepdims=True)
    ot_s[...] = jnp.zeros_like(ot_s)

    def weigh(c, sums):
        at = pl.ds(pl.multiple_of(c * CHUNK, CHUNK), CHUNK)
        e = jnp.exp(e_s[at, :] - largest)
        e_s[at, :] = e
        ot_s[...] += mm(kv_s[at, pl.ds(128, 128)], e.astype(bf16), ((0,), (0,)))
        return sums + jnp.sum(e.reshape(CHUNK // 8, 8, lanes), axis=0)

    sums = lax.fori_loop(0, chunks, weigh, jnp.zeros((8, lanes), f32))
    inverse = 1.0 / jnp.sum(sums, axis=0, keepdims=True)
    out_t = ot_s[...] * inverse
    delta = jnp.sum(g2t.astype(f32) * out_t, axis=0, keepdims=True)
    dqt_s[...] = jnp.zeros_like(dqt_s)
    dwkv_s[...] = jnp.zeros_like(dwkv_s)

    def back(c, carry):
        at = pl.ds(pl.multiple_of(c * CHUNK, CHUNK), CHUNK)
        kv = kv_s[at, :]
        probs = e_s[at, :] * inverse
        dscore = (probs * (mm(kv[:, 128:], g2t) - delta)).astype(bf16)
        dqt_s[...] += mm(kv[:, :128], dscore, ((0,), (0,)))
        dkv = jnp.concatenate([mm(dscore, q2), mm(probs.astype(bf16), g2)], axis=1).astype(bf16)
        dh_s[at, :] += mm(dkv, wkv, ((1,), (1,)))
        dwkv_s[...] += mm(hct[c], dkv)
        return carry

    lax.fori_loop(0, chunks, back, 0)

    def merged(stacked_t):
        stacked = stacked_t.T
        return jnp.where(low, stacked[:rows], stacked[rows:])

    attended = merged(out_t).astype(bf16)
    dquery = (merged(dqt_s[...]) * factor).astype(bf16)
    upd_s[...] += mm(attended, wo)
    dwo_ref[...] = mm(attended.T, masked[...]).astype(bf16)
    dw3_ref[0] = mm(own_t[...], dquery).astype(bf16)
    dwkv = dwkv_s[...].astype(bf16)
    dw3_ref[1] = dwkv[:, :128]
    dw3_ref[2] = dwkv[:, 128:]
    dhq_s[...] += mm(dquery, wq, ((1,), (1,)))

    @pl.when(step == pl.num_programs(0) - 1)
    def _():
        live = lax.broadcasted_iota(jnp.int32, (rows, width), 0) < own_count
        updated_ref[...] = (
            tokens[...].astype(f32) + jnp.where(live, upd_s[...], 0.0)
        ).astype(bf16)
        targets[0][...] = dhq_s[...]
        for target in targets[1:]:
            target[...] = jnp.zeros_like(target)
        offset = jnp.int32(0)
        for s, (which, start) in enumerate(segments):

            def scatter(j, carry, which=which, start=start, offset=offset):
                there = pl.multiple_of(offset + j * GROUP, GROUP)
                here = pl.multiple_of(start + j * GROUP, GROUP)
                part = dh_s[pl.ds(there, GROUP), :]
                if which == 0:
                    targets[0][pl.ds(here, GROUP), :] += part
                else:
                    targets[which][pl.ds(here, GROUP), :] = part.astype(bf16)
                return carry

            lax.fori_loop(0, meta[0, s], scatter, 0)
            offset = offset + meta[0, s] * GROUP


def layer(meta, segments, tokens, grads, sources, projections):
    rows, width = tokens.shape
    pairs = HEADS // 2
    most = sum(a.shape[0] for a in sources)
    room = -(-most // CHUNK) * CHUNK

    def whole(shape):
        return pl.BlockSpec(shape, lambda i: (0,) * len(shape))

    out_shape = (
        [
            jax.ShapeDtypeStruct((rows, width), bf16),
            jax.ShapeDtypeStruct((3, width, width), bf16),
            jax.ShapeDtypeStruct((width, width), bf16),
            jax.ShapeDtypeStruct((rows, width), f32),
        ]
        + [jax.ShapeDtypeStruct(a.shape, bf16) for a in sources[1:]]
    )
    out_specs = [
        whole((rows, width)),
        pl.BlockSpec((3, width, 128), lambda i: (0, 0, i)),
        pl.BlockSpec((128, width), lambda i: (i, 0)),
    ] + [whole(a.shape) for a in sources]
    in_specs = (
        [pl.BlockSpec(memory_space=pltpu.SMEM), whole((rows, width)), whole((rows, width))]
        + [whole(a.shape) for a in sources]
        + [pl.BlockSpec((1, width, 128), lambda i, p=p: (p, 0, i)) for p in range(3)]
        + [pl.BlockSpec((1, 128, width), lambda i: (3, i, 0))]
    )
    scratch = [
        pltpu.VMEM((room, width), bf16),
        pltpu.VMEM((room // CHUNK, width, CHUNK), bf16),
        pltpu.VMEM((width, rows), bf16),
        pltpu.VMEM((rows, width), bf16),
        pltpu.VMEM((room, 128), f32),
        pltpu.VMEM((room, 256), bf16),
        pltpu.VMEM((room, 2 * rows), f32),
        pltpu.VMEM((room, width), f32),
        pltpu.VMEM((128, 2 * rows), f32),
        pltpu.VMEM((128, 2 * rows), f32),
        pltpu.VMEM((width, 256), f32),
        pltpu.VMEM((rows, width), f32),
        pltpu.VMEM((rows, width), f32),
    ]
    return pl.pallas_call(
        functools.partial(layer_kernel, segments, len(sources)),
        grid=(pairs,),
        in_specs=in_specs,
        out_specs=out_specs,
        out_shape=out_shape,
        scratch_shapes=scratch,
        compiler_params=pltpu.CompilerParams(
            dimension_semantics=("arbitrary",), vmem_limit_bytes=60 * 1024 * 1024
        ),
        name="layer",
    )(meta, tokens, grads, *sources, projections, projections, projections, projections)


def half_of(array, index):
    size = array.shape[0] // 2
    return lax.dynamic_slice_in_dim(array, index * size, size, axis=0)


def added(left, right):
    return (left.astype(f32) + right.astype(f32)).astype(bf16)


def in_order(pieces, place):
    count = len(pieces)
    ring = jnp.stack([pieces[-m % count] for m in range(count)] * 2)
    return lax.dynamic_slice_in_dim(ring, (count - place) % count, count, axis=0)


def split_bits(peers):
    return [b for b in range(peers.bit_length() - 1)]


def fold(array, axis, bits, place):
    for b in bits:
        mine = (place >> b) & 1
        array = added(half_of(array, mine), swapped(half_of(array, 1 - mine), axis, b))
    return array


def unfold(array, axis, bits, place):
    for b in reversed(bits):
        other = swapped(array, axis, b)
        array = jnp.where(
            ((place >> b) & 1) == 1,
            jnp.concatenate([other, array], axis=0),
            jnp.concatenate([array, other], axis=0),
        )
    return array


def fold_line(arrays, axis, place):
    peers = lax.axis_size(axis)

    def part(index):
        return jnp.concatenate(
            [
                lax.dynamic_slice_in_dim(
                    a, (index % peers) * (a.shape[0] // peers), a.shape[0] // peers, axis=0
                )
                for a in arrays
            ],
            axis=0,
        )

    got = [rotated(part(place + k), axis, k) for k in range(1, peers)]
    result = part(place).astype(f32)
    for g in got:
        result = result + g.astype(f32)
    return result


def local(
    tokens, summary, counts, tile_pattern, summary_pattern, norm_gain, projections, cotangent
):
    tile = tokens.shape[2]
    width = tokens.shape[3]
    n_ty = lax.axis_size("ty")
    n_tx = lax.axis_size("tx")
    row = lax.axis_index("ty")
    col = lax.axis_index("tx")
    zero = jnp.zeros((), jnp.int32)
    rows = tokens[0, 0]
    grads = cotangent[0, 0]
    row_scale = rms_scale(rows)
    hidden = (rows.astype(f32) * row_scale * norm_gain).astype(bf16)
    summary_scale = rms_scale(summary)
    summary_hidden = (summary.astype(f32) * summary_scale * norm_gain).astype(bf16)

    up = shifted(hidden, "ty", 1)
    down = shifted(hidden, "ty", -1)
    left = shifted(hidden, "tx", 1)
    right = shifted(hidden, "tx", -1)
    bits = split_bits(n_ty)
    gathered = unfold(summary_hidden, "ty", bits[::-1], row)
    both = jnp.concatenate([up, down], axis=0)
    left_two = shifted(both, "tx", 1)
    right_two = shifted(both, "tx", -1)
    columns = [gathered] + [rotated(gathered, "tx", k) for k in range(1, n_tx)]
    each = summary.shape[0]
    every_summary = (
        in_order(columns, col)
        .reshape(n_tx, n_ty, each, width)
        .transpose(1, 0, 2, 3)
        .reshape(n_ty * n_tx * each, width)
    )

    near_counts = lax.dynamic_slice(jnp.pad(counts, 1), (row, col), (3, 3)).reshape(9)
    flags = lax.dynamic_slice(tile_pattern, (row, col, zero), (1, 1, 9)).reshape(9)
    valid = jnp.concatenate(
        [
            jnp.where(flags == 1, near_counts, 0),
            jnp.where(summary_pattern[0, 0] == 1, SBLK, 0),
        ]
    ).astype(jnp.int32)
    groups = (valid + GROUP - 1) // GROUP
    meta = jnp.stack(
        [
            jnp.concatenate([groups, jnp.sum(groups, keepdims=True) * GROUP]),
            jnp.concatenate([valid, near_counts[4:5]]),
        ]
    ).astype(jnp.int32)
    segments = (
        (5, 0), (1, 0), (6, 0),
        (3, 0), (0, 0), (4, 0),
        (5, tile), (2, 0), (6, tile),
    ) + tuple((7, SBLK * b) for b in range(summary_pattern.shape[2]))
    sources = [hidden, up, down, left, right, left_two, right_two, every_summary]
    results = layer(meta, segments, rows, grads, sources, projections)
    updated, dw3, dwo = results[:3]
    d_own, d_up, d_down, d_left, d_right, d_left_two, d_right_two, d_summary = results[3:]

    a_one = fold(dw3[0], "ty", bits, row)
    b_one = fold(dwo, "ty", bits[::-1], row)

    pair_sum = (
        jnp.concatenate([d_up, d_down], axis=0).astype(f32)
        + shifted(d_right_two, "tx", 1).astype(f32)
        + shifted(d_left_two, "tx", -1).astype(f32)
    ).astype(bf16)
    from_left = shifted(d_right, "tx", 1)
    from_right = shifted(d_left, "tx", -1)

    one = fold_line([a_one, b_one], "tx", col).astype(bf16)

    a_two = fold(dw3[1], "ty", bits, row)
    b_two = fold(dw3[2], "ty", bits[::-1], row)
    s_two = fold(d_summary, "ty", bits[::-1], row)

    from_above = shifted(pair_sum[tile:], "ty", 1)
    from_below = shifted(pair_sum[:tile], "ty", -1)
    hidden_grad = (
        d_own
        + from_left.astype(f32)
        + from_right.astype(f32)
        + from_above.astype(f32)
        + from_below.astype(f32)
    )

    two = fold_line([a_two, b_two, s_two], "tx", col)
    summary_hidden_grad = two[-each:]
    two = two[:-each].astype(bf16)

    def spread(block):
        pieces = [block] + [rotated(block, "tx", k) for k in range(1, n_tx)]
        stacked = in_order(pieces, col)
        size = block.shape[0] // 2
        a = stacked[:, :size].reshape(n_tx * size, width)
        b = stacked[:, size:].reshape(n_tx * size, width)
        return unfold(a, "ty", bits, row), unfold(b, "ty", bits[::-1], row)

    g_query, g_out = spread(one)
    g_key, g_value = spread(two)
    grad_proj = jnp.stack([g_query, g_key, g_value, g_out]).astype(f32)
    grad_gain = jnp.sum(grad_proj[:3] * projections[:3].astype(f32), axis=(0, 2)) / norm_gain
    grad_tokens = (
        grads.astype(f32) + norm_back(rows, row_scale, norm_gain, hidden_grad)
    ).astype(bf16)
    grad_summary = norm_back(summary, summary_scale, norm_gain, summary_hidden_grad).astype(bf16)
    return (
        updated.reshape(tokens.shape),
        grad_tokens.reshape(tokens.shape),
        grad_summary,
        grad_proj,
        grad_gain,
    )


def solution(mesh):
    return jax.shard_map(
        local,
        mesh=mesh,
        in_specs=(
            P(("slide", "ty"), "tx", None, None),
            P(("slide", "ty", "tx"), None),
            P("slide", None),
            P("slide", None, None),
            P(("slide", "ty"), "tx", None),
            P(),
            P(),
            P(("slide", "ty"), "tx", None, None),
        ),
        out_specs=(
            P(("slide", "ty"), "tx", None, None),
            P(("slide", "ty"), "tx", None, None),
            P(("slide", "ty", "tx"), None),
            P("slide", None, None),
            P("slide"),
        ),
        check_vma=False,
    )
```

```python
import functools
import math

import jax
import jax.numpy as jnp
from jax import lax
from jax.experimental import pallas as pl
from jax.experimental.pallas import tpu as pltpu
from jax.sharding import PartitionSpec as P


HEADS = 12
SBLK = 128
CHUNK = 256
BLOCK = 512
GROUP = 16
FAR = -1e30
epsilon = 1e-05


f32 = jnp.float32
bf16 = jnp.bfloat16


def shifted(array, axis, by):
    peers = lax.axis_size(axis)
    pairs = [(i, i + by) for i in range(peers) if 0 <= i + by < peers]
    return lax.ppermute(array, axis, pairs)


def rotated(array, axis, by):
    peers = lax.axis_size(axis)
    return lax.ppermute(array, axis, [(i, (i + by) % peers) for i in range(peers)])


def swapped(array, axis, bit):
    peers = lax.axis_size(axis)
    return lax.ppermute(array, axis, [(i, i ^ (1 << bit)) for i in range(peers)])


def rms_scale(rows):
    values = rows.astype(f32)
    return lax.rsqrt(jnp.mean(values * values, axis=-1, keepdims=True) + epsilon)


def norm_back(rows, scale, gain, grad_norm):
    values = rows.astype(f32)
    scaled = gain * grad_norm
    return scale * scaled - values * scale**3 * jnp.mean(values * scaled, axis=-1, keepdims=True)


def mm(left, right, contract=((1,), (0,))):
    return lax.dot_general(left, right, (contract, ((), ())), preferred_element_type=f32)


def layer_kernel(segments, n_in, meta, tokens, query, grad, masked, weights, *refs):
    sources = refs[:n_in]
    outs = refs[n_in:]
    updated_ref, dw_ref = outs[:2]
    targets = outs[2 : 2 + n_in]
    (hc, hct, bias, k_s, v_s, e_s, acc_s, o_s, dq_s, dw_s) = outs[2 + n_in :]
    own_ref = sources[0]
    n_seg = len(segments)
    rows = own_ref.shape[0]
    width = own_ref.shape[1]
    half = width // HEADS
    pairs = HEADS // 2
    lanes = 2 * rows
    factor = 1.0 / math.sqrt(half)
    total = meta[0, n_seg]
    chunks = lax.div(total + (CHUNK - 1), CHUNK)
    blocks = lax.div(total + (BLOCK - 1), BLOCK)
    own_count = meta[1, n_seg]

    offset = jnp.int32(0)
    for s, (which, start) in enumerate(segments):
        valid = meta[1, s]

        def gather(j, carry, which=which, start=start, valid=valid, offset=offset):
            there = pl.multiple_of(offset + j * GROUP, GROUP)
            here = pl.multiple_of(start + j * GROUP, GROUP)
            hc[pl.ds(there, GROUP), :] = sources[which][pl.ds(here, GROUP), :]
            place = lax.broadcasted_iota(jnp.int32, (GROUP, 128), 0) + j * GROUP
            bias[pl.ds(there, GROUP), :] = jnp.where(place < valid, 0.0, FAR)
            return carry

        lax.fori_loop(0, meta[0, s], gather, 0)
        offset = offset + meta[0, s] * GROUP

    def tail(j, carry):
        there = pl.multiple_of(j * GROUP, GROUP)
        hc[pl.ds(there, GROUP), :] = jnp.zeros((GROUP, width), bf16)
        bias[pl.ds(there, GROUP), :] = jnp.full((GROUP, 128), FAR, f32)
        return carry

    lax.fori_loop(lax.div(total, GROUP), blocks * (BLOCK // GROUP), tail, 0)

    def block_at(c):
        return pl.ds(pl.multiple_of(c * BLOCK, BLOCK), BLOCK)

    def chunk_at(c):
        return pl.ds(pl.multiple_of(c * CHUNK, CHUNK), CHUNK)

    def project(c, carry):
        at = block_at(c)
        h = hc[at, :]
        hct[c] = h.T
        for n in range(0, width, 256):
            k_s[at, n : n + 256] = mm(h, weights[1, :, n : n + 256]).astype(bf16)
            v_s[at, n : n + 256] = mm(h, weights[2, :, n : n + 256]).astype(bf16)
        return carry

    lax.fori_loop(0, blocks, project, 0)

    low = lax.broadcasted_iota(jnp.int32, (rows, 128), 1) < half

    def two(ref, i):
        part = ref[:, 128 * i : 128 * (i + 1)]
        nil = jnp.zeros_like(part)
        return jnp.concatenate([jnp.where(low, part, nil), jnp.where(low, nil, part)], axis=0)

    def merged(stacked_t):
        stacked = stacked_t.T
        return jnp.where(low, stacked[:rows], stacked[rows:])

    def score(i, c, q2t, largest):
        at = chunk_at(c)
        b = bias[at, :]
        scores = mm(k_s[at, 128 * i : 128 * (i + 1)], q2t)
        scores = scores + jnp.concatenate([b] * (lanes // 128), axis=1)
        e_s[i % 2, at, :] = scores
        return jnp.maximum(largest, jnp.max(scores.reshape(CHUNK // 8, 8, lanes), axis=0))

    nothing = jnp.full((8, lanes), FAR, f32)
    q2t = two(query, 0).T
    largest = lax.fori_loop(0, chunks, lambda c, m: score(0, c, q2t, m), nothing)

    for i in range(pairs):
        q2 = two(query, i)
        g2 = two(grad, i)
        g2t = g2.T
        cols = slice(128 * i, 128 * (i + 1))
        top = jnp.max(largest, axis=0, keepdims=True)
        acc_s[...] = jnp.zeros_like(acc_s)

        def weigh(c, sums):
            at = chunk_at(c)
            e = jnp.exp(e_s[i % 2, at, :] - top)
            e_s[i % 2, at, :] = e
            acc_s[...] += mm(v_s[at, cols], e.astype(bf16), ((0,), (0,)))
            return sums + jnp.sum(e.reshape(CHUNK // 8, 8, lanes), axis=0)

        sums = lax.fori_loop(0, chunks, weigh, jnp.zeros((8, lanes), f32))
        inverse = 1.0 / jnp.sum(sums, axis=0, keepdims=True)
        out_t = acc_s[...] * inverse
        delta = jnp.sum(g2t.astype(f32) * out_t, axis=0, keepdims=True)
        o_s[:, cols] = merged(out_t).astype(bf16)
        acc_s[...] = jnp.zeros_like(acc_s)
        more = i + 1 < pairs
        if more:
            q2t = two(query, i + 1).T

        def back(c, largest):
            at = chunk_at(c)
            if more:
                largest = score(i + 1, c, q2t, largest)
            probs = e_s[i % 2, at, :] * inverse
            dscore = (probs * (mm(v_s[at, cols], g2t) - delta)).astype(bf16)
            acc_s[...] += mm(k_s[at, cols], dscore, ((0,), (0,)))
            k_s[at, cols] = mm(dscore, q2).astype(bf16)
            v_s[at, cols] = mm(probs.astype(bf16), g2).astype(bf16)
            return largest

        largest = lax.fori_loop(0, chunks, back, nothing)
        dq_s[:, cols] = (merged(acc_s[...]) * factor).astype(bf16)

    own_t = own_ref[...].T
    attended = o_s[...]
    attended_t = attended.T
    dquery = dq_s[...]
    live = lax.broadcasted_iota(jnp.int32, (rows, 256), 0) < own_count
    for n in range(0, width, 256):
        cut = slice(n, n + 256)
        moved = jnp.where(live, mm(attended, weights[3, :, cut]), 0.0)
        updated_ref[:, cut] = (tokens[:, cut].astype(f32) + moved).astype(bf16)
        dw_ref[0, :, cut] = mm(own_t, dquery[:, cut]).astype(bf16)
        dw_ref[3, :, cut] = mm(attended_t, masked[:, cut]).astype(bf16)
        targets[0][:, cut] = mm(dquery, weights[0, cut, :], ((1,), (1,)))
    for source, into in ((k_s, 1), (v_s, 2)):

        def outer(c, carry, source=source, into=into):
            at = block_at(c)
            for n in range(0, width, 256):
                dw_s[:, n : n + 256] += mm(hct[c], source[at, n : n + 256])
            return carry

        dw_s[...] = jnp.zeros_like(dw_s)
        lax.fori_loop(0, blocks, outer, 0)
        dw_ref[into] = dw_s[...].astype(bf16)

    def returned(c, carry):
        at = block_at(c)
        for n in range(0, width, 256):
            cut = slice(n, n + 256)
            hc[at, cut] = (
                mm(k_s[at, :], weights[1, cut, :], ((1,), (1,)))
                + mm(v_s[at, :], weights[2, cut, :], ((1,), (1,)))
            ).astype(bf16)
        return carry

    lax.fori_loop(0, blocks, returned, 0)
    for target in targets[1:]:
        target[...] = jnp.zeros_like(target)
    offset = jnp.int32(0)
    for s, (which, start) in enumerate(segments):

        def scatter(j, carry, which=which, start=start, offset=offset):
            there = pl.multiple_of(offset + j * GROUP, GROUP)
            here = pl.multiple_of(start + j * GROUP, GROUP)
            part = hc[pl.ds(there, GROUP), :]
            if which == 0:
                targets[0][pl.ds(here, GROUP), :] += part.astype(f32)
            else:
                targets[which][pl.ds(here, GROUP), :] = part
            return carry

        lax.fori_loop(0, meta[0, s], scatter, 0)
        offset = offset + meta[0, s] * GROUP


def layer(meta, segments, tokens, query, grad, masked, sources, projections):
    rows, width = tokens.shape
    most = sum(a.shape[0] for a in sources)
    room = -(-most // BLOCK) * BLOCK
    vmem = pl.BlockSpec(memory_space=pltpu.VMEM)
    out_shape = [
        jax.ShapeDtypeStruct((rows, width), bf16),
        jax.ShapeDtypeStruct((4, width, width), bf16),
        jax.ShapeDtypeStruct((rows, width), f32),
    ] + [jax.ShapeDtypeStruct(a.shape, bf16) for a in sources[1:]]
    scratch = [
        pltpu.VMEM((room, width), bf16),
        pltpu.VMEM((room // BLOCK, width, BLOCK), bf16),
        pltpu.VMEM((room, 128), f32),
        pltpu.VMEM((room, width), bf16),
        pltpu.VMEM((room, width), bf16),
        pltpu.VMEM((2, room, 2 * rows), f32),
        pltpu.VMEM((128, 2 * rows), f32),
        pltpu.VMEM((rows, width), bf16),
        pltpu.VMEM((rows, width), bf16),
        pltpu.VMEM((width, width), f32),
    ]
    held = room * (3 * width * 2 + width * 2 + 512 + 16 * rows) + 6 * width * width * 4
    grant = held + 4 * most * width + 6 * 2**20
    return pl.pallas_call(
        functools.partial(layer_kernel, segments, len(sources)),
        in_specs=[pl.BlockSpec(memory_space=pltpu.SMEM)] + [vmem] * (5 + len(sources)),
        out_specs=[vmem] * len(out_shape),
        out_shape=out_shape,
        scratch_shapes=scratch,
        compiler_params=pltpu.CompilerParams(vmem_limit_bytes=grant),
        name="layer",
    )(meta, tokens, query, grad, masked, projections, *sources)


def half_of(array, index):
    size = array.shape[0] // 2
    return lax.dynamic_slice_in_dim(array, index * size, size, axis=0)


def added(left, right):
    return (left.astype(f32) + right.astype(f32)).astype(bf16)


def in_order(pieces, place):
    count = len(pieces)
    ring = jnp.stack([pieces[-m % count] for m in range(count)] * 2)
    return lax.dynamic_slice_in_dim(ring, (count - place) % count, count, axis=0)


def split_bits(peers):
    return [b for b in range(peers.bit_length() - 1)]


def fold(arrays, axis, b, place):
    mine = (place >> b) & 1
    sent = [half_of(a, 1 - mine) for a in arrays]
    got = swapped(sent[0] if len(sent) == 1 else jnp.concatenate(sent, axis=0), axis, b)
    kept, start = [], 0
    for a in arrays:
        size = a.shape[0] // 2
        kept.append(added(half_of(a, mine), got[start : start + size]))
        start += size
    return kept


def unfold(array, axis, b, place):
    other = swapped(array, axis, b)
    return jnp.where(
        ((place >> b) & 1) == 1,
        jnp.concatenate([other, array], axis=0),
        jnp.concatenate([array, other], axis=0),
    )


def fold_line(arrays, axis, place):
    peers = lax.axis_size(axis)

    def part(index):
        return jnp.concatenate(
            [
                lax.dynamic_slice_in_dim(
                    a, (index % peers) * (a.shape[0] // peers), a.shape[0] // peers, axis=0
                )
                for a in arrays
            ],
            axis=0,
        )

    got = [rotated(part(place + k), axis, k) for k in range(1, peers)]
    result = part(place).astype(f32)
    for g in got:
        result = result + g.astype(f32)
    return result


def after(value, *others):
    return lax.optimization_barrier((value,) + others)[0]


def local(
    tokens, summary, counts, tile_pattern, summary_pattern, norm_gain, projections, cotangent
):
    tile = tokens.shape[2]
    width = tokens.shape[3]
    n_ty = lax.axis_size("ty")
    n_tx = lax.axis_size("tx")
    row = lax.axis_index("ty")
    col = lax.axis_index("tx")
    zero = jnp.zeros((), jnp.int32)
    rows = tokens[0, 0]
    grads = cotangent[0, 0]
    row_scale = rms_scale(rows)
    hidden = (rows.astype(f32) * row_scale * norm_gain).astype(bf16)
    summary_scale = rms_scale(summary)
    summary_hidden = (summary.astype(f32) * summary_scale * norm_gain).astype(bf16)

    bits = split_bits(n_ty)
    back_bits = bits[::-1]
    gathered = summary_hidden
    for b in bits:
        gathered = unfold(gathered, "ty", b, row)
    up = shifted(hidden, "ty", 1)
    down = shifted(hidden, "ty", -1)
    left = shifted(hidden, "tx", 1)
    right = shifted(hidden, "tx", -1)
    columns = [gathered]
    for k in range(1, n_tx):
        columns.append(rotated(gathered, "tx", k))
    both = jnp.concatenate([up, down], axis=0)
    left_two = shifted(both, "tx", 1)
    right_two = shifted(both, "tx", -1)
    each = summary.shape[0]
    every_summary = (
        in_order(columns, col)
        .reshape(n_tx, n_ty, each, width)
        .transpose(1, 0, 2, 3)
        .reshape(n_ty * n_tx * each, width)
    )

    live = jnp.arange(tile, dtype=jnp.int32)[:, None] < lax.dynamic_slice(
        counts, (row, col), (1, 1)
    )
    masked = jnp.where(live, grads, jnp.zeros_like(grads))
    factor = 1.0 / math.sqrt(width // HEADS)
    query = (mm(hidden, projections[0]).astype(bf16) * factor).astype(bf16)
    grad = mm(masked, projections[3], ((1,), (1,))).astype(bf16)
    near_counts = lax.dynamic_slice(jnp.pad(counts, 1), (row, col), (3, 3)).reshape(9)
    flags = lax.dynamic_slice(tile_pattern, (row, col, zero), (1, 1, 9)).reshape(9)
    valid = jnp.concatenate(
        [
            jnp.where(flags == 1, near_counts, 0),
            jnp.where(summary_pattern[0, 0] == 1, SBLK, 0),
        ]
    ).astype(jnp.int32)
    groups = (valid + GROUP - 1) // GROUP
    meta = jnp.stack(
        [
            jnp.concatenate([groups, jnp.sum(groups, keepdims=True) * GROUP]),
            jnp.concatenate([valid, near_counts[4:5]]),
        ]
    ).astype(jnp.int32)
    segments = (
        (5, 0), (1, 0), (6, 0),
        (3, 0), (0, 0), (4, 0),
        (5, tile), (2, 0), (6, tile),
    ) + tuple((7, SBLK * b) for b in range(summary_pattern.shape[2]))
    sources = [hidden, up, down, left, right, left_two, right_two, every_summary]
    results = layer(meta, segments, rows, query, grad, masked, sources, projections)
    updated, dw = results[:2]
    d_own, d_up, d_down, d_left, d_right, d_left_two, d_right_two, d_summary = results[2:]

    def halves(left_list, right_list, level):
        return (
            fold(left_list, "ty", bits[level], row),
            fold(right_list, "ty", back_bits[level], row),
        )

    one = ([dw[0]], [dw[3]])
    one = halves(*one, 0)
    far_right = shifted(d_right_two, "tx", 1)
    far_left = shifted(d_left_two, "tx", -1)
    from_left = shifted(d_right, "tx", 1)
    from_right = shifted(d_left, "tx", -1)
    two = ([after(dw[1], *one[0])], [after(dw[2], *one[1]), d_summary])
    two = halves(*two, 0)
    for level in range(1, len(bits)):
        one = halves(*one, level)
    for level in range(1, len(bits)):
        two = halves(*two, level)
    one = fold_line(one[0] + one[1], "tx", col).astype(bf16)
    pair_sum = (
        jnp.concatenate([d_up, d_down], axis=0).astype(f32)
        + far_right.astype(f32)
        + far_left.astype(f32)
    ).astype(bf16)
    pair_sum = after(pair_sum, *two[0])
    from_above = shifted(pair_sum[tile:], "ty", 1)
    from_below = shifted(pair_sum[:tile], "ty", -1)
    hidden_grad = (
        d_own
        + from_left.astype(f32)
        + from_right.astype(f32)
        + from_above.astype(f32)
        + from_below.astype(f32)
    )
    two = fold_line(two[0] + two[1], "tx", col)
    summary_hidden_grad = two[-each:]
    two = two[:-each].astype(bf16)

    def spread(block):
        pieces = [block] + [rotated(block, "tx", k) for k in range(1, n_tx)]
        stacked = in_order(pieces, col)
        size = block.shape[0] // 2
        a = stacked[:, :size].reshape(n_tx * size, width)
        b = stacked[:, size:].reshape(n_tx * size, width)
        for level in reversed(range(len(bits))):
            a = unfold(a, "ty", bits[level], row)
            b = unfold(b, "ty", back_bits[level], row)
        return a, b

    g_query, g_out = spread(one)
    g_key, g_value = spread(two)
    grad_proj = jnp.stack([g_query, g_key, g_value, g_out]).astype(f32)
    grad_gain = jnp.sum(grad_proj[:3] * projections[:3].astype(f32), axis=(0, 2)) / norm_gain
    grad_tokens = (
        grads.astype(f32) + norm_back(rows, row_scale, norm_gain, hidden_grad)
    ).astype(bf16)
    grad_summary = norm_back(summary, summary_scale, norm_gain, summary_hidden_grad).astype(bf16)
    return (
        updated.reshape(tokens.shape),
        grad_tokens.reshape(tokens.shape),
        grad_summary,
        grad_proj,
        grad_gain,
    )


def solution(mesh):
    return jax.shard_map(
        local,
        mesh=mesh,
        in_specs=(
            P(("slide", "ty"), "tx", None, None),
            P(("slide", "ty", "tx"), None),
            P("slide", None),
            P("slide", None, None),
            P(("slide", "ty"), "tx", None),
            P(),
            P(),
            P(("slide", "ty"), "tx", None, None),
        ),
        out_specs=(
            P(("slide", "ty"), "tx", None, None),
            P(("slide", "ty"), "tx", None, None),
            P(("slide", "ty", "tx"), None),
            P("slide", None, None),
            P("slide"),
        ),
        check_vma=False,
    )
```

```python
import functools
import math

import jax
import jax.numpy as jnp
from jax import lax
from jax.experimental import pallas as pl
from jax.experimental.pallas import tpu as pltpu
from jax.sharding import PartitionSpec as P


HEADS = 12
SBLK = 128
CHUNK = 256
BLOCK = 512
GROUP = 16
FAR = -1e30
epsilon = 1e-05


f32 = jnp.float32
bf16 = jnp.bfloat16


def shifted(array, axis, by):
    peers = lax.axis_size(axis)
    pairs = [(i, i + by) for i in range(peers) if 0 <= i + by < peers]
    return lax.ppermute(array, axis, pairs)


def rotated(array, axis, by):
    peers = lax.axis_size(axis)
    return lax.ppermute(array, axis, [(i, (i + by) % peers) for i in range(peers)])


def swapped(array, axis, bit):
    peers = lax.axis_size(axis)
    return lax.ppermute(array, axis, [(i, i ^ (1 << bit)) for i in range(peers)])


def rms_scale(rows):
    values = rows.astype(f32)
    return lax.rsqrt(jnp.mean(values * values, axis=-1, keepdims=True) + epsilon)


def norm_back(rows, scale, gain, grad_norm):
    values = rows.astype(f32)
    scaled = gain * grad_norm
    return scale * scaled - values * scale**3 * jnp.mean(values * scaled, axis=-1, keepdims=True)


def mm(left, right, contract=((1,), (0,))):
    return lax.dot_general(left, right, (contract, ((), ())), preferred_element_type=f32)


def layer_kernel(segments, n_in, meta, tokens, query, grad, masked, weights, *refs):
    sources = refs[:n_in]
    outs = refs[n_in:]
    updated_ref = outs[0]
    dw_refs = outs[1:5]
    targets = outs[5 : 5 + n_in]
    (hc, hct, bias, k_s, v_s, e_s, p_s, acc_s, o_s, dq_s, dw_s) = outs[5 + n_in :]
    own_ref = sources[0]
    n_seg = len(segments)
    rows = own_ref.shape[0]
    width = own_ref.shape[1]
    half = width // HEADS
    pairs = HEADS // 2
    lanes = 2 * rows
    factor = 1.0 / math.sqrt(half)
    total = meta[0, n_seg]
    chunks = lax.div(total + (CHUNK - 1), CHUNK)
    blocks = lax.div(total + (BLOCK - 1), BLOCK)
    own_count = meta[1, n_seg]

    offset = jnp.int32(0)
    for s, (which, start) in enumerate(segments):
        valid = meta[1, s]

        def gather(j, carry, which=which, start=start, valid=valid, offset=offset):
            there = pl.multiple_of(offset + j * GROUP, GROUP)
            here = pl.multiple_of(start + j * GROUP, GROUP)
            hc[pl.ds(there, GROUP), :] = sources[which][pl.ds(here, GROUP), :]
            place = lax.broadcasted_iota(jnp.int32, (GROUP, 128), 0) + j * GROUP
            bias[pl.ds(there, GROUP), :] = jnp.where(place < valid, 0.0, FAR)
            return carry

        lax.fori_loop(0, meta[0, s], gather, 0)
        offset = offset + meta[0, s] * GROUP

    def tail(j, carry):
        there = pl.multiple_of(j * GROUP, GROUP)
        hc[pl.ds(there, GROUP), :] = jnp.zeros((GROUP, width), bf16)
        bias[pl.ds(there, GROUP), :] = jnp.full((GROUP, 128), FAR, f32)
        return carry

    lax.fori_loop(lax.div(total, GROUP), blocks * (BLOCK // GROUP), tail, 0)

    def block_at(c):
        return pl.ds(pl.multiple_of(c * BLOCK, BLOCK), BLOCK)

    def chunk_at(c):
        return pl.ds(pl.multiple_of(c * CHUNK, CHUNK), CHUNK)

    def project(c, carry):
        at = block_at(c)
        h = hc[at, :]
        hct[c] = h.T
        for n in range(0, width, 256):
            k_s[at, n : n + 256] = mm(h, weights[1, :, n : n + 256]).astype(bf16)
            v_s[at, n : n + 256] = mm(h, weights[2, :, n : n + 256]).astype(bf16)
        return carry

    lax.fori_loop(0, blocks, project, 0)

    low = lax.broadcasted_iota(jnp.int32, (rows, 128), 1) < half

    def two(ref, i):
        part = ref[:, 128 * i : 128 * (i + 1)]
        nil = jnp.zeros_like(part)
        return jnp.concatenate([jnp.where(low, part, nil), jnp.where(low, nil, part)], axis=0)

    def merged(stacked_t):
        stacked = stacked_t.T
        return jnp.where(low, stacked[:rows], stacked[rows:])

    def score(i, c, q2t, largest):
        at = chunk_at(c)
        b = bias[at, :]
        scores = mm(k_s[at, 128 * i : 128 * (i + 1)], q2t)
        scores = scores + jnp.concatenate([b] * (lanes // 128), axis=1)
        e_s[i % 2, at, :] = scores
        return jnp.maximum(largest, jnp.max(scores.reshape(CHUNK // 8, 8, lanes), axis=0))

    nothing = jnp.full((8, lanes), FAR, f32)
    q2t = two(query, 0).T
    largest = lax.fori_loop(0, chunks, lambda c, m: score(0, c, q2t, m), nothing)

    for i in range(pairs):
        q2 = two(query, i)
        g2 = two(grad, i)
        g2t = g2.T
        cols = slice(128 * i, 128 * (i + 1))
        top = jnp.max(largest, axis=0, keepdims=True)
        acc_s[...] = jnp.zeros_like(acc_s)

        def weigh(c, sums):
            at = chunk_at(c)
            e = jnp.exp(e_s[i % 2, at, :] - top)
            e_s[i % 2, at, :] = e
            p_s[at, :] = mm(v_s[at, cols], g2t)
            acc_s[...] += mm(v_s[at, cols], e.astype(bf16), ((0,), (0,)))
            return sums + jnp.sum(e.reshape(CHUNK // 8, 8, lanes), axis=0)

        sums = lax.fori_loop(0, chunks, weigh, jnp.zeros((8, lanes), f32))
        inverse = 1.0 / jnp.sum(sums, axis=0, keepdims=True)
        out_t = acc_s[...] * inverse
        delta = jnp.sum(g2t.astype(f32) * out_t, axis=0, keepdims=True)
        o_s[:, cols] = merged(out_t).astype(bf16)
        acc_s[...] = jnp.zeros_like(acc_s)
        more = i + 1 < pairs
        if more:
            q2t = two(query, i + 1).T

        def back(c, largest):
            at = chunk_at(c)
            if more:
                largest = score(i + 1, c, q2t, largest)
            probs = e_s[i % 2, at, :] * inverse
            dscore = (probs * (p_s[at, :] - delta)).astype(bf16)
            acc_s[...] += mm(k_s[at, cols], dscore, ((0,), (0,)))
            k_s[at, cols] = mm(dscore, q2).astype(bf16)
            v_s[at, cols] = mm(probs.astype(bf16), g2).astype(bf16)
            return largest

        largest = lax.fori_loop(0, chunks, back, nothing)
        dq_s[:, cols] = (merged(acc_s[...]) * factor).astype(bf16)

    own_t = own_ref[...].T
    attended = o_s[...]
    attended_t = attended.T
    dquery = dq_s[...]
    live = lax.broadcasted_iota(jnp.int32, (rows, 256), 0) < own_count
    for n in range(0, width, 256):
        cut = slice(n, n + 256)
        moved = jnp.where(live, mm(attended, weights[3, :, cut]), 0.0)
        updated_ref[:, cut] = (tokens[:, cut].astype(f32) + moved).astype(bf16)
        dw_refs[0][:, cut] = mm(own_t, dquery[:, cut]).astype(bf16)
        dw_refs[3][:, cut] = mm(attended_t, masked[:, cut]).astype(bf16)
        targets[0][:, cut] = mm(dquery, weights[0, cut, :], ((1,), (1,)))
    for source, into in ((k_s, 1), (v_s, 2)):

        def outer(c, carry, source=source, into=into):
            at = block_at(c)
            for n in range(0, width, 256):
                dw_s[:, n : n + 256] += mm(hct[c], source[at, n : n + 256])
            return carry

        dw_s[...] = jnp.zeros_like(dw_s)
        lax.fori_loop(0, blocks, outer, 0)
        dw_refs[into][...] = dw_s[...].astype(bf16)

    def returned(c, carry):
        at = block_at(c)
        for n in range(0, width, 256):
            cut = slice(n, n + 256)
            hc[at, cut] = (
                mm(k_s[at, :], weights[1, cut, :], ((1,), (1,)))
                + mm(v_s[at, :], weights[2, cut, :], ((1,), (1,)))
            ).astype(bf16)
        return carry

    lax.fori_loop(0, blocks, returned, 0)
    for target in targets[1:]:
        target[...] = jnp.zeros_like(target)
    offset = jnp.int32(0)
    for s, (which, start) in enumerate(segments):

        def scatter(j, carry, which=which, start=start, offset=offset):
            there = pl.multiple_of(offset + j * GROUP, GROUP)
            here = pl.multiple_of(start + j * GROUP, GROUP)
            part = hc[pl.ds(there, GROUP), :]
            if which == 0:
                targets[0][pl.ds(here, GROUP), :] += part.astype(f32)
            else:
                targets[which][pl.ds(here, GROUP), :] = part
            return carry

        lax.fori_loop(0, meta[0, s], scatter, 0)
        offset = offset + meta[0, s] * GROUP


def layer(meta, segments, tokens, query, grad, masked, sources, projections):
    rows, width = tokens.shape
    most = sum(a.shape[0] for a in sources)
    room = -(-most // BLOCK) * BLOCK
    vmem = pl.BlockSpec(memory_space=pltpu.VMEM)
    out_shape = [
        jax.ShapeDtypeStruct((rows, width), bf16),
        *[jax.ShapeDtypeStruct((width, width), bf16)] * 4,
        jax.ShapeDtypeStruct((rows, width), f32),
    ] + [jax.ShapeDtypeStruct(a.shape, bf16) for a in sources[1:]]
    scratch = [
        pltpu.VMEM((room, width), bf16),
        pltpu.VMEM((room // BLOCK, width, BLOCK), bf16),
        pltpu.VMEM((room, 128), f32),
        pltpu.VMEM((room, width), bf16),
        pltpu.VMEM((room, width), bf16),
        pltpu.VMEM((2, room, 2 * rows), f32),
        pltpu.VMEM((room, 2 * rows), f32),
        pltpu.VMEM((128, 2 * rows), f32),
        pltpu.VMEM((rows, width), bf16),
        pltpu.VMEM((rows, width), bf16),
        pltpu.VMEM((width, width), f32),
    ]
    held = room * (3 * width * 2 + width * 2 + 512 + 24 * rows) + 6 * width * width * 4
    grant = held + 4 * most * width + 6 * 2**20
    return pl.pallas_call(
        functools.partial(layer_kernel, segments, len(sources)),
        in_specs=[pl.BlockSpec(memory_space=pltpu.SMEM)] + [vmem] * (5 + len(sources)),
        out_specs=[vmem] * len(out_shape),
        out_shape=out_shape,
        scratch_shapes=scratch,
        compiler_params=pltpu.CompilerParams(vmem_limit_bytes=grant),
        name="layer",
    )(meta, tokens, query, grad, masked, projections, *sources)


def half_of(array, index):
    size = array.shape[0] // 2
    return lax.dynamic_slice_in_dim(array, index * size, size, axis=0)


def added(left, right):
    return (left.astype(f32) + right.astype(f32)).astype(bf16)


def in_order(pieces, place):
    count = len(pieces)
    ring = jnp.stack([pieces[-m % count] for m in range(count)] * 2)
    return lax.dynamic_slice_in_dim(ring, (count - place) % count, count, axis=0)


def split_bits(peers):
    return [b for b in range(peers.bit_length() - 1)]


def fold(arrays, axis, b, place):
    mine = (place >> b) & 1
    sent = [half_of(a, 1 - mine) for a in arrays]
    got = swapped(sent[0] if len(sent) == 1 else jnp.concatenate(sent, axis=0), axis, b)
    kept, start = [], 0
    for a in arrays:
        size = a.shape[0] // 2
        kept.append(added(half_of(a, mine), got[start : start + size]))
        start += size
    return kept


def unfold(array, axis, b, place):
    other = swapped(array, axis, b)
    return jnp.where(
        ((place >> b) & 1) == 1,
        jnp.concatenate([other, array], axis=0),
        jnp.concatenate([array, other], axis=0),
    )


def fold_line(arrays, axis, place):
    peers = lax.axis_size(axis)

    def part(index):
        return jnp.concatenate(
            [
                lax.dynamic_slice_in_dim(
                    a, (index % peers) * (a.shape[0] // peers), a.shape[0] // peers, axis=0
                )
                for a in arrays
            ],
            axis=0,
        )

    got = [rotated(part(place + k), axis, k) for k in range(1, peers)]
    result = part(place).astype(f32)
    for g in got:
        result = result + g.astype(f32)
    return result


def after(value, *others):
    return lax.optimization_barrier((value,) + others)[0]


def local(
    tokens, summary, counts, tile_pattern, summary_pattern, norm_gain, projections, cotangent
):
    tile = tokens.shape[2]
    width = tokens.shape[3]
    n_ty = lax.axis_size("ty")
    n_tx = lax.axis_size("tx")
    row = lax.axis_index("ty")
    col = lax.axis_index("tx")
    zero = jnp.zeros((), jnp.int32)
    rows = tokens[0, 0]
    grads = cotangent[0, 0]
    row_scale = rms_scale(rows)
    hidden = (rows.astype(f32) * row_scale * norm_gain).astype(bf16)
    summary_scale = rms_scale(summary)
    summary_hidden = (summary.astype(f32) * summary_scale * norm_gain).astype(bf16)

    bits = split_bits(n_ty)
    back_bits = bits[::-1]
    up = shifted(hidden, "ty", 1)
    down = shifted(hidden, "ty", -1)
    left = shifted(hidden, "tx", 1)
    right = shifted(hidden, "tx", -1)
    columns = [summary_hidden]
    for k in range(1, n_tx):
        columns.append(rotated(summary_hidden, "tx", k))
    both = jnp.concatenate([up, down], axis=0)
    left_two = shifted(both, "tx", 1)
    right_two = shifted(both, "tx", -1)
    each = summary.shape[0]
    every_summary = in_order(columns, col).reshape(n_tx * each, width)
    for b in bits:
        every_summary = unfold(every_summary, "ty", b, row)

    live = jnp.arange(tile, dtype=jnp.int32)[:, None] < lax.dynamic_slice(
        counts, (row, col), (1, 1)
    )
    masked = jnp.where(live, grads, jnp.zeros_like(grads))
    factor = 1.0 / math.sqrt(width // HEADS)
    query = (mm(hidden, projections[0]).astype(bf16) * factor).astype(bf16)
    grad = mm(masked, projections[3], ((1,), (1,))).astype(bf16)
    near_counts = lax.dynamic_slice(jnp.pad(counts, 1), (row, col), (3, 3)).reshape(9)
    flags = lax.dynamic_slice(tile_pattern, (row, col, zero), (1, 1, 9)).reshape(9)
    valid = jnp.concatenate(
        [
            jnp.where(flags == 1, near_counts, 0),
            jnp.where(summary_pattern[0, 0] == 1, SBLK, 0),
        ]
    ).astype(jnp.int32)
    groups = (valid + GROUP - 1) // GROUP
    meta = jnp.stack(
        [
            jnp.concatenate([groups, jnp.sum(groups, keepdims=True) * GROUP]),
            jnp.concatenate([valid, near_counts[4:5]]),
        ]
    ).astype(jnp.int32)
    segments = (
        (5, 0), (1, 0), (6, 0),
        (3, 0), (0, 0), (4, 0),
        (5, tile), (2, 0), (6, tile),
    ) + tuple((7, SBLK * b) for b in range(summary_pattern.shape[2]))
    sources = [hidden, up, down, left, right, left_two, right_two, every_summary]
    results = layer(meta, segments, rows, query, grad, masked, sources, projections)
    updated, dw = results[0], results[1:5]
    d_own, d_up, d_down, d_left, d_right, d_left_two, d_right_two, d_summary = results[5:]

    def halves(left_list, right_list, level):
        return (
            fold(left_list, "ty", bits[level], row),
            fold(right_list, "ty", back_bits[level], row),
        )

    one = ([dw[0]], [dw[3]])
    one = halves(*one, 0)
    far_right = shifted(d_right_two, "tx", 1)
    far_left = shifted(d_left_two, "tx", -1)
    from_left = shifted(d_right, "tx", 1)
    from_right = shifted(d_left, "tx", -1)
    two = ([after(dw[1], *one[0])], [after(dw[2], *one[1]), d_summary])
    two = halves(*two, 0)
    for level in range(1, len(bits)):
        one = halves(*one, level)
    for level in range(1, len(bits)):
        two = halves(*two, level)
    one = fold_line(one[0] + one[1], "tx", col).astype(bf16)
    pair_sum = (
        jnp.concatenate([d_up, d_down], axis=0).astype(f32)
        + far_right.astype(f32)
        + far_left.astype(f32)
    ).astype(bf16)
    pair_sum = after(pair_sum, *two[0], *two[1])
    from_above = shifted(pair_sum[tile:], "ty", 1)
    from_below = shifted(pair_sum[:tile], "ty", -1)
    hidden_grad = (
        d_own
        + from_left.astype(f32)
        + from_right.astype(f32)
        + from_above.astype(f32)
        + from_below.astype(f32)
    )
    folded = two[0] + two[1]
    two = fold_line(folded, "tx", col)
    summary_hidden_grad = two[-each:]
    two = two[:-each].astype(bf16)

    def spread(block, *wait):
        pieces = [block]
        for k in range(1, n_tx):
            pieces.append(rotated(block, "tx", k))
        stacked = in_order(pieces, col)
        if wait:
            stacked = after(stacked, *wait)
        size = block.shape[0] // 2
        a = stacked[:, :size].reshape(n_tx * size, width)
        b = stacked[:, size:].reshape(n_tx * size, width)
        for level in reversed(range(len(bits))):
            a = unfold(a, "ty", bits[level], row)
            b = unfold(b, "ty", back_bits[level], row)
        return a, b

    g_query, g_out = spread(one, *folded)
    g_key, g_value = spread(two)
    grad_proj = jnp.stack([g_query, g_key, g_value, g_out]).astype(f32)
    grad_gain = jnp.sum(grad_proj[:3] * projections[:3].astype(f32), axis=(0, 2)) / norm_gain
    grad_tokens = (
        grads.astype(f32) + norm_back(rows, row_scale, norm_gain, hidden_grad)
    ).astype(bf16)
    grad_summary = norm_back(summary, summary_scale, norm_gain, summary_hidden_grad).astype(bf16)
    return (
        updated.reshape(tokens.shape),
        grad_tokens.reshape(tokens.shape),
        grad_summary,
        grad_proj,
        grad_gain,
    )


def solution(mesh):
    return jax.shard_map(
        local,
        mesh=mesh,
        in_specs=(
            P(("slide", "ty"), "tx", None, None),
            P(("slide", "ty", "tx"), None),
            P("slide", None),
            P("slide", None, None),
            P(("slide", "ty"), "tx", None),
            P(),
            P(),
            P(("slide", "ty"), "tx", None, None),
        ),
        out_specs=(
            P(("slide", "ty"), "tx", None, None),
            P(("slide", "ty"), "tx", None, None),
            P(("slide", "ty", "tx"), None),
            P("slide", None, None),
            P("slide"),
        ),
        check_vma=False,
    )
```

```python
import functools
import math

import jax
import jax.numpy as jnp
from jax import lax
from jax.experimental import pallas as pl
from jax.experimental.pallas import tpu as pltpu
from jax.sharding import PartitionSpec as P


HEADS = 12
SBLK = 128
CHUNK = 256
BLOCK = 512
GROUP = 16
FAR = -1e30
epsilon = 1e-05


f32 = jnp.float32
bf16 = jnp.bfloat16


def shifted(array, axis, by):
    peers = lax.axis_size(axis)
    pairs = [(i, i + by) for i in range(peers) if 0 <= i + by < peers]
    return lax.ppermute(array, axis, pairs)


def rotated(array, axis, by):
    peers = lax.axis_size(axis)
    return lax.ppermute(array, axis, [(i, (i + by) % peers) for i in range(peers)])


def swapped(array, axis, bit):
    peers = lax.axis_size(axis)
    return lax.ppermute(array, axis, [(i, i ^ (1 << bit)) for i in range(peers)])


def rms_scale(rows):
    values = rows.astype(f32)
    return lax.rsqrt(jnp.mean(values * values, axis=-1, keepdims=True) + epsilon)


def norm_back(rows, scale, gain, grad_norm):
    values = rows.astype(f32)
    scaled = gain * grad_norm
    return scale * scaled - values * scale**3 * jnp.mean(values * scaled, axis=-1, keepdims=True)


def mm(left, right, contract=((1,), (0,))):
    return lax.dot_general(left, right, (contract, ((), ())), preferred_element_type=f32)


def layer_kernel(segments, n_in, meta, tokens, query, grad, masked, weights, *refs):
    sources = refs[:n_in]
    outs = refs[n_in:]
    updated_ref = outs[0]
    dw_refs = outs[1:5]
    targets = outs[5 : 5 + n_in]
    (hc, hct, bias, k_s, v_s, e_s, p_s, acc_s, o_s, dq_s, dw_s) = outs[5 + n_in :]
    own_ref = sources[0]
    n_seg = len(segments)
    rows = own_ref.shape[0]
    width = own_ref.shape[1]
    half = width // HEADS
    pairs = HEADS // 2
    lanes = 2 * rows
    factor = 1.0 / math.sqrt(half)
    total = meta[0, n_seg]
    chunks = lax.div(total + (CHUNK - 1), CHUNK)
    blocks = lax.div(total + (BLOCK - 1), BLOCK)
    own_count = meta[1, n_seg]

    offset = jnp.int32(0)
    for s, (which, start) in enumerate(segments):
        valid = meta[1, s]

        def gather(j, carry, which=which, start=start, valid=valid, offset=offset):
            there = pl.multiple_of(offset + j * GROUP, GROUP)
            here = pl.multiple_of(start + j * GROUP, GROUP)
            hc[pl.ds(there, GROUP), :] = sources[which][pl.ds(here, GROUP), :]
            place = lax.broadcasted_iota(jnp.int32, (GROUP, 128), 0) + j * GROUP
            bias[pl.ds(there, GROUP), :] = jnp.where(place < valid, 0.0, FAR)
            return carry

        lax.fori_loop(0, meta[0, s], gather, 0)
        offset = offset + meta[0, s] * GROUP

    def tail(j, carry):
        there = pl.multiple_of(j * GROUP, GROUP)
        hc[pl.ds(there, GROUP), :] = jnp.zeros((GROUP, width), bf16)
        bias[pl.ds(there, GROUP), :] = jnp.full((GROUP, 128), FAR, f32)
        return carry

    lax.fori_loop(lax.div(total, GROUP), blocks * (BLOCK // GROUP), tail, 0)

    def block_at(c):
        return pl.ds(pl.multiple_of(c * BLOCK, BLOCK), BLOCK)

    def chunk_at(c):
        return pl.ds(pl.multiple_of(c * CHUNK, CHUNK), CHUNK)

    def project(c, carry):
        at = block_at(c)
        h = hc[at, :]
        hct[c] = h.T
        for n in range(0, width, 256):
            k_s[at, n : n + 256] = mm(h, weights[1, :, n : n + 256]).astype(bf16)
            v_s[at, n : n + 256] = mm(h, weights[2, :, n : n + 256]).astype(bf16)
        return carry

    lax.fori_loop(0, blocks, project, 0)

    low = lax.broadcasted_iota(jnp.int32, (rows, 128), 1) < half

    def two(ref, i):
        part = ref[:, 128 * i : 128 * (i + 1)]
        nil = jnp.zeros_like(part)
        return jnp.concatenate([jnp.where(low, part, nil), jnp.where(low, nil, part)], axis=0)

    def merged(stacked_t):
        stacked = stacked_t.T
        return jnp.where(low, stacked[:rows], stacked[rows:])

    def score(i, c, q2t, largest):
        at = chunk_at(c)
        b = bias[at, :]
        scores = mm(k_s[at, 128 * i : 128 * (i + 1)], q2t)
        scores = scores + jnp.concatenate([b] * (lanes // 128), axis=1)
        e_s[i % 2, at, :] = scores
        return jnp.maximum(largest, jnp.max(scores.reshape(CHUNK // 8, 8, lanes), axis=0))

    nothing = jnp.full((8, lanes), FAR, f32)
    q2t = two(query, 0).T
    largest = lax.fori_loop(0, chunks, lambda c, m: score(0, c, q2t, m), nothing)

    for i in range(pairs):
        q2 = two(query, i)
        g2 = two(grad, i)
        g2t = g2.T
        cols = slice(128 * i, 128 * (i + 1))
        top = jnp.max(largest, axis=0, keepdims=True)
        acc_s[...] = jnp.zeros_like(acc_s)

        def weigh(c, sums):
            at = chunk_at(c)
            e = jnp.exp(e_s[i % 2, at, :] - top)
            e_s[i % 2, at, :] = e
            p_s[at, :] = mm(v_s[at, cols], g2t)
            acc_s[...] += mm(v_s[at, cols], e.astype(bf16), ((0,), (0,)))
            return sums + jnp.sum(e.reshape(CHUNK // 8, 8, lanes), axis=0)

        sums = lax.fori_loop(0, chunks, weigh, jnp.zeros((8, lanes), f32))
        inverse = 1.0 / jnp.sum(sums, axis=0, keepdims=True)
        out_t = acc_s[...] * inverse
        delta = jnp.sum(g2t.astype(f32) * out_t, axis=0, keepdims=True)
        o_s[:, cols] = merged(out_t).astype(bf16)
        acc_s[...] = jnp.zeros_like(acc_s)
        more = i + 1 < pairs
        if more:
            q2t = two(query, i + 1).T

        def back(c, largest):
            at = chunk_at(c)
            if more:
                largest = score(i + 1, c, q2t, largest)
            probs = e_s[i % 2, at, :] * inverse
            dscore = (probs * (p_s[at, :] - delta)).astype(bf16)
            acc_s[...] += mm(k_s[at, cols], dscore, ((0,), (0,)))
            k_s[at, cols] = mm(dscore, q2).astype(bf16)
            v_s[at, cols] = mm(probs.astype(bf16), g2).astype(bf16)
            return largest

        largest = lax.fori_loop(0, chunks, back, nothing)
        dq_s[:, cols] = (merged(acc_s[...]) * factor).astype(bf16)

    own_t = own_ref[...].T
    attended = o_s[...]
    attended_t = attended.T
    dquery = dq_s[...]
    live = lax.broadcasted_iota(jnp.int32, (rows, 256), 0) < own_count
    for n in range(0, width, 256):
        cut = slice(n, n + 256)
        moved = jnp.where(live, mm(attended, weights[3, :, cut]), 0.0)
        updated_ref[:, cut] = (tokens[:, cut].astype(f32) + moved).astype(bf16)
        dw_refs[0][:, cut] = mm(own_t, dquery[:, cut]).astype(bf16)
        dw_refs[3][:, cut] = mm(attended_t, masked[:, cut]).astype(bf16)
        targets[0][:, cut] = mm(dquery, weights[0, cut, :], ((1,), (1,)))
    for source, into in ((k_s, 1), (v_s, 2)):

        def outer(c, carry, source=source, into=into):
            at = block_at(c)
            for n in range(0, width, 256):
                dw_s[:, n : n + 256] += mm(hct[c], source[at, n : n + 256])
            return carry

        dw_s[...] = jnp.zeros_like(dw_s)
        lax.fori_loop(0, blocks, outer, 0)
        dw_refs[into][...] = dw_s[...].astype(bf16)

    def returned(c, carry):
        at = block_at(c)
        for n in range(0, width, 256):
            cut = slice(n, n + 256)
            hc[at, cut] = (
                mm(k_s[at, :], weights[1, cut, :], ((1,), (1,)))
                + mm(v_s[at, :], weights[2, cut, :], ((1,), (1,)))
            ).astype(bf16)
        return carry

    lax.fori_loop(0, blocks, returned, 0)
    for target in targets[1:]:
        target[...] = jnp.zeros_like(target)
    offset = jnp.int32(0)
    for s, (which, start) in enumerate(segments):

        def scatter(j, carry, which=which, start=start, offset=offset):
            there = pl.multiple_of(offset + j * GROUP, GROUP)
            here = pl.multiple_of(start + j * GROUP, GROUP)
            part = hc[pl.ds(there, GROUP), :]
            if which == 0:
                targets[0][pl.ds(here, GROUP), :] += part.astype(f32)
            else:
                targets[which][pl.ds(here, GROUP), :] = part
            return carry

        lax.fori_loop(0, meta[0, s], scatter, 0)
        offset = offset + meta[0, s] * GROUP


def layer(meta, segments, tokens, query, grad, masked, sources, projections):
    rows, width = tokens.shape
    most = sum(a.shape[0] for a in sources)
    room = -(-most // BLOCK) * BLOCK
    vmem = pl.BlockSpec(memory_space=pltpu.VMEM)
    out_shape = [
        jax.ShapeDtypeStruct((rows, width), bf16),
        *[jax.ShapeDtypeStruct((width, width), bf16)] * 4,
        jax.ShapeDtypeStruct((rows, width), f32),
    ] + [jax.ShapeDtypeStruct(a.shape, bf16) for a in sources[1:]]
    scratch = [
        pltpu.VMEM((room, width), bf16),
        pltpu.VMEM((room // BLOCK, width, BLOCK), bf16),
        pltpu.VMEM((room, 128), f32),
        pltpu.VMEM((room, width), bf16),
        pltpu.VMEM((room, width), bf16),
        pltpu.VMEM((2, room, 2 * rows), f32),
        pltpu.VMEM((room, 2 * rows), f32),
        pltpu.VMEM((128, 2 * rows), f32),
        pltpu.VMEM((rows, width), bf16),
        pltpu.VMEM((rows, width), bf16),
        pltpu.VMEM((width, width), f32),
    ]
    held = room * (3 * width * 2 + width * 2 + 512 + 24 * rows) + 6 * width * width * 4
    grant = held + 4 * most * width + 6 * 2**20
    return pl.pallas_call(
        functools.partial(layer_kernel, segments, len(sources)),
        in_specs=[pl.BlockSpec(memory_space=pltpu.SMEM)] + [vmem] * (5 + len(sources)),
        out_specs=[vmem] * len(out_shape),
        out_shape=out_shape,
        scratch_shapes=scratch,
        compiler_params=pltpu.CompilerParams(vmem_limit_bytes=grant),
        name="layer",
    )(meta, tokens, query, grad, masked, projections, *sources)


def half_of(array, index):
    size = array.shape[0] // 2
    return lax.dynamic_slice_in_dim(array, index * size, size, axis=0)


def added(left, right):
    return (left.astype(f32) + right.astype(f32)).astype(bf16)


def in_order(pieces, place):
    count = len(pieces)
    ring = jnp.stack([pieces[-m % count] for m in range(count)] * 2)
    return lax.dynamic_slice_in_dim(ring, (count - place) % count, count, axis=0)


def split_bits(peers):
    return [b for b in range(peers.bit_length() - 1)]


def fold(arrays, axis, b, place):
    mine = (place >> b) & 1
    sent = [half_of(a, 1 - mine) for a in arrays]
    got = swapped(sent[0] if len(sent) == 1 else jnp.concatenate(sent, axis=0), axis, b)
    kept, start = [], 0
    for a in arrays:
        size = a.shape[0] // 2
        kept.append(added(half_of(a, mine), got[start : start + size]))
        start += size
    return kept


def unfold(array, axis, b, place):
    other = swapped(array, axis, b)
    return jnp.where(
        ((place >> b) & 1) == 1,
        jnp.concatenate([other, array], axis=0),
        jnp.concatenate([array, other], axis=0),
    )


def fold_line(arrays, axis, place):
    peers = lax.axis_size(axis)

    def part(index):
        return jnp.concatenate(
            [
                lax.dynamic_slice_in_dim(
                    a, (index % peers) * (a.shape[0] // peers), a.shape[0] // peers, axis=0
                )
                for a in arrays
            ],
            axis=0,
        )

    got = [rotated(part(place + k), axis, k) for k in range(1, peers)]
    result = part(place).astype(f32)
    for g in got:
        result = result + g.astype(f32)
    return result


def after(value, *others):
    return lax.optimization_barrier((value,) + others)[0]


def local(
    tokens, summary, counts, tile_pattern, summary_pattern, norm_gain, projections, cotangent
):
    tile = tokens.shape[2]
    width = tokens.shape[3]
    n_ty = lax.axis_size("ty")
    n_tx = lax.axis_size("tx")
    row = lax.axis_index("ty")
    col = lax.axis_index("tx")
    zero = jnp.zeros((), jnp.int32)
    rows = tokens[0, 0]
    grads = cotangent[0, 0]
    row_scale = rms_scale(rows)
    hidden = (rows.astype(f32) * row_scale * norm_gain).astype(bf16)
    summary_scale = rms_scale(summary)
    summary_hidden = (summary.astype(f32) * summary_scale * norm_gain).astype(bf16)

    bits = split_bits(n_ty)
    back_bits = bits[::-1]
    up = shifted(hidden, "ty", 1)
    down = shifted(hidden, "ty", -1)
    left = shifted(hidden, "tx", 1)
    right = shifted(hidden, "tx", -1)
    columns = [summary_hidden]
    for k in range(1, n_tx):
        columns.append(rotated(summary_hidden, "tx", k))
    both = jnp.concatenate([up, down], axis=0)
    each = summary.shape[0]
    every_summary = in_order(columns, col).reshape(n_tx * each, width)
    for b in bits:
        every_summary = unfold(every_summary, "ty", b, row)

    own, grads_in, counts, both = lax.optimization_barrier((hidden, grads, counts, both))
    left_two = shifted(both, "tx", 1)
    right_two = shifted(both, "tx", -1)
    live = jnp.arange(tile, dtype=jnp.int32)[:, None] < lax.dynamic_slice(
        counts, (row, col), (1, 1)
    )
    masked = jnp.where(live, grads_in, jnp.zeros_like(grads_in))
    factor = 1.0 / math.sqrt(width // HEADS)
    query = (mm(own, projections[0]).astype(bf16) * factor).astype(bf16)
    grad = mm(masked, projections[3], ((1,), (1,))).astype(bf16)
    near_counts = lax.dynamic_slice(jnp.pad(counts, 1), (row, col), (3, 3)).reshape(9)
    flags = lax.dynamic_slice(tile_pattern, (row, col, zero), (1, 1, 9)).reshape(9)
    valid = jnp.concatenate(
        [
            jnp.where(flags == 1, near_counts, 0),
            jnp.where(summary_pattern[0, 0] == 1, SBLK, 0),
        ]
    ).astype(jnp.int32)
    groups = (valid + GROUP - 1) // GROUP
    meta = jnp.stack(
        [
            jnp.concatenate([groups, jnp.sum(groups, keepdims=True) * GROUP]),
            jnp.concatenate([valid, near_counts[4:5]]),
        ]
    ).astype(jnp.int32)
    segments = (
        (5, 0), (1, 0), (6, 0),
        (3, 0), (0, 0), (4, 0),
        (5, tile), (2, 0), (6, tile),
    ) + tuple((7, SBLK * b) for b in range(summary_pattern.shape[2]))
    sources = [hidden, up, down, left, right, left_two, right_two, every_summary]
    results = layer(meta, segments, rows, query, grad, masked, sources, projections)
    updated, dw = results[0], results[1:5]
    d_own, d_up, d_down, d_left, d_right, d_left_two, d_right_two, d_summary = results[5:]

    def halves(left_list, right_list, level):
        return (
            fold(left_list, "ty", bits[level], row),
            fold(right_list, "ty", back_bits[level], row),
        )

    one = ([dw[0]], [dw[3]])
    one = halves(*one, 0)
    far_right = shifted(d_right_two, "tx", 1)
    far_left = shifted(d_left_two, "tx", -1)
    from_left = shifted(d_right, "tx", 1)
    from_right = shifted(d_left, "tx", -1)
    two = ([after(dw[1], *one[0])], [after(dw[2], *one[1]), d_summary])
    two = halves(*two, 0)
    for level in range(1, len(bits)):
        one = halves(*one, level)
    for level in range(1, len(bits)):
        two = halves(*two, level)
    one = fold_line(one[0] + one[1], "tx", col).astype(bf16)
    pair_sum = (
        jnp.concatenate([d_up, d_down], axis=0).astype(f32)
        + far_right.astype(f32)
        + far_left.astype(f32)
    ).astype(bf16)
    pair_sum = after(pair_sum, *two[0], *two[1])
    from_above = shifted(pair_sum[tile:], "ty", 1)
    from_below = shifted(pair_sum[:tile], "ty", -1)
    hidden_grad = (
        d_own
        + from_left.astype(f32)
        + from_right.astype(f32)
        + from_above.astype(f32)
        + from_below.astype(f32)
    )
    folded = two[0] + two[1]
    two = fold_line(folded, "tx", col)
    summary_hidden_grad = two[-each:]
    two = two[:-each].astype(bf16)

    def spread(block, *wait):
        pieces = [block]
        for k in range(1, n_tx):
            pieces.append(rotated(block, "tx", k))
        stacked = in_order(pieces, col)
        if wait:
            stacked = after(stacked, *wait)
        size = block.shape[0] // 2
        a = stacked[:, :size].reshape(n_tx * size, width)
        b = stacked[:, size:].reshape(n_tx * size, width)
        for level in reversed(range(len(bits))):
            a = unfold(a, "ty", bits[level], row)
            b = unfold(b, "ty", back_bits[level], row)
        return a, b

    g_query, g_out = spread(one, *folded)
    g_key, g_value = spread(two)
    grad_proj = jnp.stack([g_query, g_key, g_value, g_out]).astype(f32)
    grad_gain = jnp.sum(grad_proj[:3] * projections[:3].astype(f32), axis=(0, 2)) / norm_gain
    grad_tokens = (
        grads.astype(f32) + norm_back(rows, row_scale, norm_gain, hidden_grad)
    ).astype(bf16)
    grad_summary = norm_back(summary, summary_scale, norm_gain, summary_hidden_grad).astype(bf16)
    return (
        updated.reshape(tokens.shape),
        grad_tokens.reshape(tokens.shape),
        grad_summary,
        grad_proj,
        grad_gain,
    )


def solution(mesh):
    return jax.shard_map(
        local,
        mesh=mesh,
        in_specs=(
            P(("slide", "ty"), "tx", None, None),
            P(("slide", "ty", "tx"), None),
            P("slide", None),
            P("slide", None, None),
            P(("slide", "ty"), "tx", None),
            P(),
            P(),
            P(("slide", "ty"), "tx", None, None),
        ),
        out_specs=(
            P(("slide", "ty"), "tx", None, None),
            P(("slide", "ty"), "tx", None, None),
            P(("slide", "ty", "tx"), None),
            P("slide", None, None),
            P("slide"),
        ),
        check_vma=False,
    )
```
